32 devices in a mesh: groups: 2 (over y), rows: 4 (over z), cols: 2 (over x), sub: 2 (over core).
Axes of the slice: x: 2, y: 2, z: 4, core: 2. Of those that a mesh axis runs over, the one named last changes fastest.
Arguments:
- data_rows: bfloat16 [16384, 256], P(('groups', 'rows')), parts along dimension 0, may hold values from -6 to 6
- landmarks: bfloat16 [4096, 256], P(('groups', 'rows', 'cols')), parts along dimension 0, may hold values from -6 to 6
- factor: bfloat16 [4096, 2048], P(('groups', 'rows', 'cols'), 'sub'), parts along dimension 0, may hold values from -0.02734375 to 0.02734375
- chosen_owner: int32 [2048, 1], P('groups'), parts along dimension 0, may hold values from 0 to 3; in each aligned block of 256 rows (0 to 255, 256 to 511, ...) at most 256 rows name the same one
- chosen_local: int32 [2048], P('groups'), parts along dimension 0, may hold values from 0 to 2047
Outputs:
- leverage: float32 [16384], P(('groups', 'rows', 'cols')), parts along dimension 0
- panel: float32 [2048, 256], P(('groups', 'rows'), 'cols'), parts along dimension 0
The draws below stay inside these ranges and needn't reach their ends.
There are 2 independent parts, one for each index of `groups`. The reference program is written for one: setup_inputs(seed, part) draws one part's arguments, and reference() takes and returns one part's arrays. A program takes and returns all parts, laid end to end along the dimension named above; each array names one. Nothing has to cross between parts.
Inputs may be any that keep to these rules, and one draw needn't show every extreme that they name: `chosen_owner`: in each aligned block of 256 chosen rows no owner appears more than 256 times, and in some block one owner appears exactly 256 times.
All inputs are finite; a program needn't handle non-finite values.
Results may differ from the reference program's by a relative error of at most 0.00039.
Values may be sent and summed in bfloat16 or wider, within the bound.
A program may use at most 64 MiB of HBM per device.

```python
import math
import jax
import jax.numpy as jnp
import numpy as np
from jax import lax

D = 256
M = 2048
SLAB = 2048
CHOSEN_DEV = 256
PANEL_DEV = 64
N = 8192
M2 = 1024
PANEL = 256
PCD = 32
OWNERS = 4
MOST = 256
N_ROWS = 4
N_COLS = 2


def with_ends(entries, key, low, top_value):
    index_at = [jax.random.randint(jax.random.fold_in(key, axis), (), 0, length) for axis, length in enumerate(entries.shape)]
    widest = entries.shape.index(max(entries.shape))
    next_to = index_at[:widest] + [(index_at[widest] + 1) % entries.shape[widest]] + index_at[widest + 1:]
    return entries.at[tuple(index_at)].set(low).at[tuple(next_to)].set(top_value)


def steps_of(rng, extent, pieces, least, top_value):
    gain, own = 1.0, jax.random.fold_in(rng, 6)
    for axis_at, shards_of in pieces:
        heights = jnp.exp(jax.random.uniform(jax.random.fold_in(own, axis_at), (shards_of,), jnp.float32, least / len(pieces), top_value / len(pieces)))
        gain = gain * jnp.repeat(heights, extent[axis_at] // shards_of).reshape([-1 if axis == axis_at else 1 for axis in range(len(extent))])
    return gain


def routed_block(key, own, number, rows, count, top, bound, skew):
    order = jax.random.permutation(key, count)
    heavy_load, ordinary = portions_of(count, rows * top, bound, skew, True), portions_of(count, rows * top, bound, skew, False)
    places = jnp.arange(count)

    def named(tallies, offset_by):
        used = int((tallies > 0).sum())
        fixed = max(1, used // 4)
        shifted = fixed + (places - fixed + offset_by * (used - fixed)) % max(1, count - fixed)
        return jnp.zeros((count,), jnp.int32).at[order[jnp.where(places < fixed, places, shifted)]].set(jnp.asarray(tallies, jnp.int32))

    tallies = jnp.where(number % 4 == 0, named(heavy_load, number // 4), named(ordinary, number - number // 4 - 1))
    mixed = jax.random.permutation(jax.random.fold_in(own, 3), count)
    source_of, sink = mixed[0:count // 2 * 2:2], mixed[1:count // 2 * 2:2]
    room = jnp.minimum(tallies[source_of] - 1, bound - tallies[sink]) // 2
    room = jnp.where((source_of == order[0]) | (sink == order[0]) | (tallies[sink] == 0), 0, jnp.maximum(room, 0))
    shifted = jax.random.randint(jax.random.fold_in(own, 4), (count // 2,), 0, 1 << 20) % (room + 1)
    tallies = tallies.at[source_of].add(-shifted).at[sink].add(shifted)
    items = jnp.searchsorted(jnp.cumsum(tallies), jnp.arange(rows * top), side="right").astype(jnp.int32)
    grid = items.reshape(top, rows).T
    grid = grid[jax.random.permutation(jax.random.fold_in(own, 1), rows)]
    offset_by = jax.random.randint(jax.random.fold_in(own, 2), (rows, 1), 0, top)
    return jnp.take_along_axis(grid, (jnp.arange(top)[None, :] + offset_by) % top, axis=1)


def portions_of(amount, total, bound, skew, full):
    weights = [(1 << 20) // math.isqrt(grade ** skew) + 1 for grade in range(1, amount + 1)]
    largest = bound if full else min(bound, max(-(-total // amount), total * weights[0] // sum(weights)))
    least = 1 if total - largest >= amount - 1 else 0
    counts, spare = [largest] + [least] * (amount - 1), total - largest - least * (amount - 1)
    while spare > 0:
        candidates = [i for i in range(1, amount) if counts[i] < largest] or [i for i in range(1, amount) if counts[i] < bound]
        mass, budget = sum([weights[i] for i in candidates]), spare
        for i in candidates:
            addition = min(bound - counts[i], max(1, budget * weights[i] // mass), spare)
            counts[i] = counts[i] + addition
            spare = spare - addition
    return np.array(counts)


def noise(rng, extent, spread, most, shards=(), dtype=jnp.bfloat16):
    values = spread * jax.random.normal(rng, extent, jnp.float32)
    if shards:
        values = values * steps_of(rng, extent, shards, -0.22, 0.18)
    return jnp.clip(values, -most, most).astype(dtype)


def setup_inputs(seed: int = 0, part: int = 0) -> dict:
    splits = jax.random.split(jax.random.key(seed), 6)
    part_keys = jax.random.split(jax.random.fold_in(splits[5], part), 6)
    data_rows = noise(part_keys[0], (N, D), 1.0, 6.0, ((0, 4),))
    landmarks = noise(part_keys[1], (M, D), 1.0, 6.0, ((0, 8),))
    factor = noise(part_keys[2], (M, M), (3.7 / M), 0.02734375, ((0, 8), (1, 2)))
    chosen_owner_keys = jax.random.split(jax.random.fold_in(part_keys[3], 1), M2 // CHOSEN_DEV)
    chosen_owner_turns = jax.random.permutation(jax.random.fold_in(part_keys[3], 3), M2 // CHOSEN_DEV)
    chosen_owner = jax.vmap(lambda own, number: routed_block(jax.random.fold_in(part_keys[3], 2), own, number, CHOSEN_DEV, OWNERS, 1, MOST, 2))(chosen_owner_keys, chosen_owner_turns).reshape((M2, 1))
    chosen_local = with_ends(jax.random.randint(part_keys[4], (M2,), 0, SLAB), jax.random.fold_in(part_keys[4], 1), 0, SLAB - 1).astype(jnp.int32)
    return {"data_rows": data_rows, "landmarks": landmarks, "factor": factor, "chosen_owner": chosen_owner, "chosen_local": chosen_local}


def kernel_values(left, right, rate_value, depth):
    left_sq = lax.optimization_barrier(jnp.sum(jnp.square(left.astype(jnp.float32)), axis=1))
    right_sq = lax.optimization_barrier(jnp.sum(jnp.square(right.astype(jnp.float32)), axis=1))
    cross = jnp.dot(left, right.T, preferred_element_type=jnp.float32)
    distance = left_sq[:, None] + right_sq[None, :] - 2.0 * cross
    return jnp.exp(rate_value * (2.0 * depth - distance))

def reference(data_rows, landmarks, factor, chosen_owner, chosen_local):
    rate_value = 0.3 / math.sqrt(8.0 * D)
    block_rows = math.gcd(N, 1024)
    blocks = data_rows.reshape(-1, block_rows, D)

    def block_total(block):
        values = kernel_values(block, landmarks, rate_value, D).astype(jnp.bfloat16)
        projected = jnp.dot(values, factor, preferred_element_type=jnp.float32)
        return lax.optimization_barrier(jnp.sum(projected * projected, axis=1))
    approx = lax.map(block_total, blocks).reshape(-1)
    leverage = (math.exp(2.0 * rate_value * D) - approx) / 8.0
    index_rows = (chosen_owner[:, 0] * SLAB + chosen_local).astype(jnp.int32)
    chosen = jnp.take(data_rows, index_rows, axis=0)
    column_grid = chosen.reshape(N_ROWS, CHOSEN_DEV, D)[:, :PANEL_DEV]
    column_grid = column_grid.reshape(N_ROWS, N_COLS, PCD, D).transpose(1, 0, 2, 3).reshape(PANEL, D)
    panel = kernel_values(chosen, column_grid, rate_value, D)
    return (leverage, panel)
```

```python
import functools
import math

import jax
import jax.numpy as jnp
from jax import lax
from jax.experimental import pallas as pl
from jax.experimental.pallas import tpu as pltpu
from jax.sharding import PartitionSpec as P

PANEL_DEV = 64
LOG2E = math.log2(math.e)
NT = (((1,), (1,)), ((), ()))


def lane_norms(block):
    sq = jnp.square(block.astype(jnp.float32))
    return lane_sums(sq)


def lane_sums(values):
    part = values[:, :128]
    for at in range(128, values.shape[1], 128):
        part = part + values[:, at:at + 128]
    return jnp.sum(part.T, axis=0, keepdims=True)


def kernel(dims, data_ref, land_ref, factor_ref, sel_ref, lev_ref, panel_ref,
           lbuf, fbuf, xbuf, dbuf, gbuf, abuf, chbuf, pbuf, tot, tbuf, cross, acc, lsq,
           lsem, fsem, xsem, dsem, asem, csem, psem, tsem, lcl, ss):
    R, C, S = dims
    NP = R // 2
    SL, D = data_ref.shape
    Lb = land_ref.shape[0]
    W = factor_ref.shape[1] // C
    SLC = SL // C
    NQ = C * S
    Qs = abuf.shape[1]
    PCD = pbuf.shape[1]
    rate = 0.3 / math.sqrt(8.0 * D)
    k = rate * LOG2E
    g = lax.axis_index("groups")
    r = lax.axis_index("rows")
    c = lax.axis_index("cols")
    s = lax.axis_index("sub")
    pair = r // 2
    par = lax.rem(r, 2)
    own = s == par
    other = s != par
    pending = []

    def send(src, dst, rsem, dev, cond=None):
        at = ss.at[len(pending)]
        copy = pltpu.make_async_remote_copy(
            src_ref=src, dst_ref=dst, send_sem=at, recv_sem=rsem,
            device_id=(g,) + tuple(dev), device_id_type=pl.DeviceIdType.MESH)
        pending.append((copy, cond))
        if cond is None:
            copy.start()
        else:
            pl.when(cond)(copy.start)

    def local(src, dst, sem, cond=None):
        copy = pltpu.make_async_copy(src, dst, sem)
        if cond is None:
            copy.start()
        else:
            pl.when(cond)(copy.start)

    def arrive(slot, sem, cond=None):
        copy = pltpu.make_async_copy(slot, slot, sem)
        if cond is None:
            copy.wait()
        else:
            pl.when(cond)(copy.wait)

    def pair_row(e, parity):
        return lax.rem(pair + e, NP) * 2 + parity

    def col_at(j):
        return lax.rem(c + j, C)

    barrier = pltpu.get_barrier_semaphore()

    def greet(i, carry):
        ri = i // NQ
        rest = lax.rem(i, NQ)
        pl.semaphore_signal(barrier, inc=1, device_id=(g, ri, rest // S, lax.rem(rest, S)),
                            device_id_type=pl.DeviceIdType.MESH)
        return carry

    lax.fori_loop(0, R * NQ, greet, 0)
    pl.semaphore_wait(barrier, R * NQ)

    mate = par + pair * 2 + 1 - 2 * par
    local(land_ref, lbuf.at[0, par, c], lcl.at[0])
    for e in range(1, NP):
        send(land_ref, lbuf.at[NP - e, s, c], lsem.at[NP - e, s, c], (pair_row(e, par), c, s), own)
    send(land_ref, lbuf.at[0, s, c], lsem.at[0, s, c], (mate, c, s), own)
    for j in range(1, C):
        send(land_ref, lbuf.at[0, s, c], lsem.at[0, s, c], (r, col_at(j), s), own)
    part = pl.ds(pl.multiple_of(c * SLC, SLC), SLC)
    send(data_ref.at[part], dbuf.at[c], dsem.at[c], (mate, c, s), own)
    for j in range(C):
        at = col_at(j)
        rows = pl.ds(pl.multiple_of(at * SLC, SLC), SLC)
        local(data_ref.at[rows], dbuf.at[at], dsem.at[at], own)
    for j in range(1, C):
        at = col_at(j)
        send(factor_ref.at[:, pl.ds(pl.multiple_of(at * W, W), W)], xbuf.at[c], xsem.at[c], (r, at, s))

    def spread(src, c0):
        for e in list(range(1, NP)) + [0]:
            slot = (NP - e) % NP
            cond = None if e else other
            send(src, fbuf.at[slot, par, c0], fsem.at[slot, par, c0], (pair_row(e, s), c, par), cond)
        local(src, fbuf.at[0, par, c0], fsem.at[0, par, c0], own)

    spread(factor_ref.at[:, pl.ds(pl.multiple_of(c * W, W), W)], c)

    per = min(R, max(1, 256 // Qs))

    def gather(i, carry):
        rows = pl.ds(pl.multiple_of(i * per * Qs, per * Qs), per * Qs)
        target = sel_ref[rows]
        lanes = lax.broadcasted_iota(jnp.int32, (per * Qs, SL), 1)
        hot = jnp.where(lanes == target, 1.0, 0.0).astype(jnp.bfloat16)
        got = jnp.dot(hot, data_ref[...], preferred_element_type=jnp.float32)
        gbuf[pl.ds(i * per, per)] = got.astype(jnp.bfloat16).reshape(per, Qs, D)
        return carry

    lax.fori_loop(0, R // per, gather, 0)
    for e in range(1, R):
        to = lax.rem(r + e, R)
        send(gbuf.at[to], abuf.at[R - e], asem.at[R - e], (to, c, s))

    arrive(lbuf.at[0, par, c], lcl.at[0])
    for d in range(NP):
        arrive(lbuf.at[d, s, c], lsem.at[d, s, c], other if d == 0 else None)
        block = lbuf.at[d, s, c]
        if d:
            send(block, block, lsem.at[d, s, c], (mate, c, s), own)
        for j in range(1, C):
            send(block, block, lsem.at[d, s, c], (r, col_at(j), s), None if d else other)
        send(block, block, lsem.at[d, s, c], (r, c, 1 - s), None if d else other)
    for d in range(NP):
        for j in range(1, C):
            at = col_at(j)
            arrive(lbuf.at[d, s, at], lsem.at[d, s, at])
            block = lbuf.at[d, s, at]
            send(block, block, lsem.at[d, s, at], (r, c, 1 - s))

    for j in range(1, C):
        at = col_at(j)
        arrive(xbuf.at[at], xsem.at[at])
        spread(xbuf.at[at], at)

    q = c * S + s
    total = gbuf[r].astype(jnp.float32)
    for e in range(1, R):
        arrive(abuf.at[R - e], asem.at[R - e])
        total = total + abuf[R - e].astype(jnp.float32)
    chbuf[q] = total.astype(jnp.bfloat16)
    for e in range(1, NQ):
        to = lax.rem(q + e, NQ)
        send(chbuf.at[q], chbuf.at[q], csem.at[q], (r, to // S, lax.rem(to, S)))

    for d in range(NP):
        for j in range(C):
            at = col_at(j)
            arrive(lbuf.at[d, 1 - s, at], lsem.at[d, 1 - s, at], own if d == 0 and j == 0 else None)
    arrive(dbuf.at[c], dsem.at[c])
    for j in range(1, C):
        send(dbuf.at[c], dbuf.at[c], dsem.at[c], (r, col_at(j), s), other)

    LM = R * C * Lb
    lands = lbuf.reshape(LM, D)
    LC = min(512, LM)
    for at in range(0, LM, LC):
        lsq[:, at:at + LC] = lane_norms(lands[at:at + LC]) * (-k)

    RB = min(256, SLC)

    def values_of(at):
        def body(i, carry):
            rows = pl.ds(pl.multiple_of(i * RB, RB), RB)
            block = dbuf[at, rows]
            up = block.astype(jnp.float32)
            bias = (2.0 * D - jnp.sum(up * up, axis=1, keepdims=True)) * k
            for lo in range(0, LM, LC):
                x = lax.dot_general(block, lands[lo:lo + LC], NT, preferred_element_type=jnp.float32)
                cross[at, rows, lo:lo + LC] = jnp.exp2(x * (2.0 * k) + (bias + lsq[:, lo:lo + LC])).astype(jnp.bfloat16)
            return carry

        lax.fori_loop(0, SLC // RB, body, 0)

    values_of(c)

    for e in range(1, NQ):
        at = lax.rem(q + e, NQ)
        arrive(chbuf.at[at], csem.at[at])
    flat = chbuf.reshape(NQ * Qs, D)
    piece = pl.ds(pl.multiple_of(c * PCD, PCD), PCD)
    for e in range(1, R):
        to = lax.rem(r + e, R)
        send(flat.at[piece], pbuf.at[r], psem.at[r], (to, c, s))
    local(flat.at[piece], pbuf.at[r], psem.at[r])

    for j in range(1, C):
        at = col_at(j)
        arrive(dbuf.at[at], dsem.at[at])
        values_of(at)

    for e in range(R):
        at = lax.rem(r + e, R)
        arrive(pbuf.at[at], psem.at[at])
    rows_in = flat[...]
    cols_in = pbuf[...].reshape(R * PCD, D)
    up = rows_in.astype(jnp.float32)
    bias = (2.0 * D - jnp.sum(up * up, axis=1, keepdims=True)) * k
    x = lax.dot_general(rows_in, cols_in, NT, preferred_element_type=jnp.float32)
    panel_ref[...] = jnp.exp2(x * (2.0 * k) + (bias - k * lane_norms(cols_in)))

    def take(d):
        for j in range(C):
            at = col_at(j)
            arrive(fbuf.at[d, s, at], fsem.at[d, s, at])
            block = fbuf.at[d, s, at]
            send(block, block, fsem.at[d, s, at], (r, c, 1 - s))
        for j in range(C):
            at = col_at(j)
            arrive(fbuf.at[d, 1 - s, at], fsem.at[d, 1 - s, at])

    KA = 2 * C * Lb
    flat_f = fbuf.reshape(LM, W)
    take(0)

    def first(i, carry):
        rows = pl.ds(pl.multiple_of(lax.rem(i, SLC // RB) * RB, RB), RB)
        at = i // (SLC // RB)
        acc[at, rows] = jnp.dot(cross[at, rows, :KA], flat_f[:KA], preferred_element_type=jnp.float32)
        return carry

    lax.fori_loop(0, SL // RB, first, 0)
    for d in range(1, NP):
        take(d)

    def last(i, carry):
        start = pl.multiple_of(lax.rem(i, SLC // RB) * RB, RB)
        rows = pl.ds(start, RB)
        at = i // (SLC // RB)
        proj = acc[at, rows]
        if NP > 1:
            proj = proj + jnp.dot(cross[at, rows, KA:], flat_f[KA:], preferred_element_type=jnp.float32)
        tot[at, :, rows] = lane_sums(proj * proj)
        return carry

    lax.fori_loop(0, SL // RB, last, 0)

    mine = par * C + c
    for j in range(C):
        at = col_at(j)
        for flip in range(2):
            core = s if flip == 0 else 1 - s
            cond = other if j == 0 and flip == 0 else None
            send(tot.at[at], tbuf.at[mine], tsem.at[mine], (pair * 2 + s, at, core), cond)
    local(tot.at[c], tbuf.at[mine], tsem.at[mine], own)
    approx = jnp.zeros((1, SLC), jnp.float32)
    for i in range(2 * C):
        arrive(tbuf.at[i], tsem.at[i])
        approx = approx + tbuf[i]
    lev_ref[...] = (math.exp(2.0 * rate * D) - approx) / 8.0
    for copy, cond in pending:
        if cond is None:
            copy.wait_send()
        else:
            pl.when(cond)(copy.wait_send)


def shards(dims, data_rows, landmarks, factor, chosen_owner, chosen_local):
    R, C, S = dims
    NP = R // 2
    SL, D = data_rows.shape
    Lb = landmarks.shape[0]
    W = factor.shape[1] // C
    NQ = C * S
    M2 = chosen_local.shape[0]
    Qs = M2 // (R * NQ)
    PCD = PANEL_DEV // C
    SLC = SL // C
    LM = R * C * Lb
    r = lax.axis_index("rows")
    q = lax.axis_index("cols") * S + lax.axis_index("sub")
    sel = jnp.where(chosen_owner[:, 0] == r, chosen_local, -1).reshape(R, NQ, Qs)
    sel = lax.dynamic_index_in_dim(sel, q, 1, keepdims=False).reshape(R * Qs, 1)
    vm = pl.BlockSpec(memory_space=pltpu.VMEM)
    bf = jnp.bfloat16
    sends = (NP - 1) + 1 + (C - 1) + 1 + (C - 1) + NP * C + (R - 1)
    sends += NP * (1 + C) + NP * (C - 1) + (NQ - 1) + (C - 1) + (R - 1) + NP * C + 2 * C
    dma = pltpu.SemaphoreType.DMA
    lev, panel = pl.pallas_call(
        functools.partial(kernel, dims),
        out_shape=(jax.ShapeDtypeStruct((1, SLC), jnp.float32),
                   jax.ShapeDtypeStruct((M2 // R, R * PCD), jnp.float32)),
        in_specs=[vm] * 4,
        out_specs=(vm, vm),
        scratch_shapes=[
            pltpu.VMEM((NP, 2, C, Lb, D), bf),
            pltpu.VMEM((NP, 2, C, Lb, W), bf),
            pltpu.VMEM((C, Lb, W), bf),
            pltpu.VMEM((C, SLC, D), bf),
            pltpu.VMEM((R, Qs, D), bf),
            pltpu.VMEM((R, Qs, D), bf),
            pltpu.VMEM((NQ, Qs, D), bf),
            pltpu.VMEM((R, PCD, D), bf),
            pltpu.VMEM((C, 1, SLC), jnp.float32),
            pltpu.VMEM((2 * C, 1, SLC), jnp.float32),
            pltpu.VMEM((C, SLC, LM), bf),
            pltpu.VMEM((C, SLC, W), jnp.float32),
            pltpu.VMEM((1, LM), jnp.float32),
            dma((NP, 2, C)), dma((NP, 2, C)), dma((C,)), dma((C,)), dma((R,)), dma((NQ,)), dma((R,)),
            dma((2 * C,)), dma((1,)), dma((sends,)),
        ],
        compiler_params=pltpu.CompilerParams(
            collective_id=0, has_side_effects=True, vmem_limit_bytes=60 * 2**20),
        name="leverage_panel",
    )(data_rows, landmarks, factor, sel)
    return lev.reshape(SLC), panel


def solution(mesh):
    placed = (
        P(("groups", "rows"), None),
        P(("groups", "rows", "cols"), None),
        P(("groups", "rows", "cols"), "sub"),
        P("groups", None),
        P("groups"),
    )
    dims = tuple(mesh.shape[name] for name in ("rows", "cols", "sub"))
    return jax.shard_map(
        functools.partial(shards, dims),
        mesh=mesh,
        in_specs=placed,
        out_specs=(P(("groups", "rows", "cols")), P(("groups", "rows"), "cols")),
        check_vma=False,
    )
```

```python
import functools
import math

import jax
import jax.numpy as jnp
from jax import lax
from jax.experimental import pallas as pl
from jax.experimental.pallas import tpu as pltpu
from jax.sharding import PartitionSpec as P

PANEL_DEV = 64
LOG2E = math.log2(math.e)
NT = (((1,), (1,)), ((), ()))


def lane_norms(block):
    sq = jnp.square(block.astype(jnp.float32))
    return lane_sums(sq)


def lane_sums(values):
    part = values[:, :128]
    for at in range(128, values.shape[1], 128):
        part = part + values[:, at:at + 128]
    return jnp.sum(part.T, axis=0, keepdims=True)


def kernel(dims, data_ref, land_ref, factor_ref, sel_ref, lev_ref, panel_ref,
           lbuf, fbuf, xbuf, dbuf, gbuf, abuf, chbuf, pbuf, tot, tbuf, cross, acc, lsq,
           lsem, fsem, xsem, dsem, asem, csem, psem, tsem, lcl, ss):
    R, C, S = dims
    NP = R // 2
    SL, D = data_ref.shape
    Lb = land_ref.shape[0]
    W = factor_ref.shape[1] // C
    SLC = SL // C
    NQ = C * S
    Qs = abuf.shape[1]
    PCD = pbuf.shape[1]
    rate = 0.3 / math.sqrt(8.0 * D)
    k = rate * LOG2E
    g = lax.axis_index("groups")
    r = lax.axis_index("rows")
    c = lax.axis_index("cols")
    s = lax.axis_index("sub")
    pair = r // 2
    par = lax.rem(r, 2)
    own = s == par
    other = s != par
    pending = []

    def send(src, dst, rsem, dev, cond=None):
        at = ss.at[len(pending)]
        copy = pltpu.make_async_remote_copy(
            src_ref=src, dst_ref=dst, send_sem=at, recv_sem=rsem,
            device_id=(g,) + tuple(dev), device_id_type=pl.DeviceIdType.MESH)
        pending.append((copy, cond))
        if cond is None:
            copy.start()
        else:
            pl.when(cond)(copy.start)

    def local(src, dst, sem, cond=None):
        copy = pltpu.make_async_copy(src, dst, sem)
        if cond is None:
            copy.start()
        else:
            pl.when(cond)(copy.start)

    def arrive(slot, sem, cond=None):
        copy = pltpu.make_async_copy(slot, slot, sem)
        if cond is None:
            copy.wait()
        else:
            pl.when(cond)(copy.wait)

    def pair_row(e, parity):
        return lax.rem(pair + e, NP) * 2 + parity

    def col_at(j):
        return lax.rem(c + j, C)

    barrier = pltpu.get_barrier_semaphore()

    def greet(i, carry):
        ri = i // NQ
        rest = lax.rem(i, NQ)
        pl.semaphore_signal(barrier, inc=1, device_id=(g, ri, rest // S, lax.rem(rest, S)),
                            device_id_type=pl.DeviceIdType.MESH)
        return carry

    lax.fori_loop(0, R * NQ, greet, 0)
    pl.semaphore_wait(barrier, R * NQ)

    mate = par + pair * 2 + 1 - 2 * par
    local(land_ref, lbuf.at[0, par, c], lcl.at[0])
    for e in range(1, NP):
        send(land_ref, lbuf.at[NP - e, s, c], lsem.at[NP - e, s, c], (pair_row(e, par), c, s), own)
    for e in range(1, NP):
        send(land_ref, lbuf.at[NP - e, 1 - s, c], lsem.at[NP - e, 1 - s, c], (pair_row(e, 1 - par), c, 1 - s), other)
    send(land_ref, lbuf.at[0, 1 - s, c], lsem.at[0, 1 - s, c], (mate, c, 1 - s), other)
    for j in range(1, C):
        send(land_ref, lbuf.at[0, s, c], lsem.at[0, s, c], (r, col_at(j), s), own)
    for j in range(1, C):
        at = col_at(j)
        send(factor_ref.at[:, pl.ds(pl.multiple_of(at * W, W), W)], xbuf.at[c], xsem.at[c], (r, at, s))

    per = min(R, max(1, 256 // Qs))

    def gather(i, carry):
        rows = pl.ds(pl.multiple_of(i * per * Qs, per * Qs), per * Qs)
        target = sel_ref[rows]
        lanes = lax.broadcasted_iota(jnp.int32, (per * Qs, SL), 1)
        hot = jnp.where(lanes == target, 1.0, 0.0).astype(jnp.bfloat16)
        got = jnp.dot(hot, data_ref[...], preferred_element_type=jnp.float32)
        gbuf[pl.ds(i * per, per)] = got.astype(jnp.bfloat16).reshape(per, Qs, D)
        return carry

    lax.fori_loop(0, R // per, gather, 0)
    for e in range(1, R):
        to = lax.rem(r + e, R)
        send(gbuf.at[to], abuf.at[R - e], asem.at[R - e], (to, c, s))

    def spread(src, c0):
        for e in list(range(1, NP)) + [0]:
            slot = (NP - e) % NP
            cond = None if e else other
            send(src, fbuf.at[slot, par, c0], fsem.at[slot, par, c0], (pair_row(e, s), c, par), cond)
        local(src, fbuf.at[0, par, c0], fsem.at[0, par, c0], own)

    spread(factor_ref.at[:, pl.ds(pl.multiple_of(c * W, W), W)], c)

    part = pl.ds(pl.multiple_of(c * SLC, SLC), SLC)
    send(data_ref.at[part], dbuf.at[c], dsem.at[c], (mate, c, s), own)
    for j in range(C):
        at = col_at(j)
        rows = pl.ds(pl.multiple_of(at * SLC, SLC), SLC)
        local(data_ref.at[rows], dbuf.at[at], dsem.at[at], own)
    q = c * S + s
    total = gbuf[r].astype(jnp.float32)
    for e in range(1, R):
        arrive(abuf.at[R - e], asem.at[R - e])
        total = total + abuf[R - e].astype(jnp.float32)
    chbuf[q] = total.astype(jnp.bfloat16)
    for e in range(1, NQ):
        to = lax.rem(q + e, NQ)
        send(chbuf.at[q], chbuf.at[q], csem.at[q], (r, to // S, lax.rem(to, S)))

    arrive(lbuf.at[0, par, c], lcl.at[0])
    for d in range(NP):
        arrive(lbuf.at[d, s, c], lsem.at[d, s, c], other if d == 0 else None)
        block = lbuf.at[d, s, c]
        for j in range(1, C):
            send(block, block, lsem.at[d, s, c], (r, col_at(j), s), None if d else other)
        send(block, block, lsem.at[d, s, c], (r, c, 1 - s), None if d else other)
    for d in range(NP):
        for j in range(1, C):
            at = col_at(j)
            arrive(lbuf.at[d, s, at], lsem.at[d, s, at])
            block = lbuf.at[d, s, at]
            send(block, block, lsem.at[d, s, at], (r, c, 1 - s))

    for e in range(1, NQ):
        at = lax.rem(q + e, NQ)
        arrive(chbuf.at[at], csem.at[at])
    flat = chbuf.reshape(NQ * Qs, D)
    piece = pl.ds(pl.multiple_of(c * PCD, PCD), PCD)
    for e in range(1, R):
        to = lax.rem(r + e, R)
        send(flat.at[piece], pbuf.at[r], psem.at[r], (to, c, s))
    local(flat.at[piece], pbuf.at[r], psem.at[r])

    for j in range(1, C):
        at = col_at(j)
        arrive(xbuf.at[at], xsem.at[at])
        spread(xbuf.at[at], at)

    for d in range(NP):
        for j in range(C):
            at = col_at(j)
            arrive(lbuf.at[d, 1 - s, at], lsem.at[d, 1 - s, at], own if d == 0 and j == 0 else None)
    arrive(dbuf.at[c], dsem.at[c])
    for j in range(1, C):
        send(dbuf.at[c], dbuf.at[c], dsem.at[c], (r, col_at(j), s), other)

    LM = R * C * Lb
    lands = lbuf.reshape(LM, D)
    LC = min(512, LM)
    for at in range(0, LM, LC):
        lsq[:, at:at + LC] = lane_norms(lands[at:at + LC]) * (-k)

    RB = min(256, SLC)

    def values_of(at):
        def body(i, carry):
            rows = pl.ds(pl.multiple_of(i * RB, RB), RB)
            block = dbuf[at, rows]
            up = block.astype(jnp.float32)
            bias = (2.0 * D - jnp.sum(up * up, axis=1, keepdims=True)) * k
            for lo in range(0, LM, LC):
                x = lax.dot_general(block, lands[lo:lo + LC], NT, preferred_element_type=jnp.float32)
                cross[at, rows, lo:lo + LC] = jnp.exp2(x * (2.0 * k) + (bias + lsq[:, lo:lo + LC])).astype(jnp.bfloat16)
            return carry

        lax.fori_loop(0, SLC // RB, body, 0)

    values_of(c)

    for j in range(1, C):
        at = col_at(j)
        arrive(dbuf.at[at], dsem.at[at])
        values_of(at)

    for e in range(R):
        at = lax.rem(r + e, R)
        arrive(pbuf.at[at], psem.at[at])
    rows_in = flat[...]
    cols_in = pbuf[...].reshape(R * PCD, D)
    up = rows_in.astype(jnp.float32)
    bias = (2.0 * D - jnp.sum(up * up, axis=1, keepdims=True)) * k
    x = lax.dot_general(rows_in, cols_in, NT, preferred_element_type=jnp.float32)
    panel_ref[...] = x * (2.0 * k) + (bias - k * lane_norms(cols_in))

    def take(d):
        for j in range(C):
            at = col_at(j)
            arrive(fbuf.at[d, s, at], fsem.at[d, s, at])
            block = fbuf.at[d, s, at]
            send(block, block, fsem.at[d, s, at], (r, c, 1 - s))
        for j in range(C):
            at = col_at(j)
            arrive(fbuf.at[d, 1 - s, at], fsem.at[d, 1 - s, at])

    KA = 2 * C * Lb
    flat_f = fbuf.reshape(LM, W)
    take(0)

    def first(i, carry):
        rows = pl.ds(pl.multiple_of(lax.rem(i, SLC // RB) * RB, RB), RB)
        at = i // (SLC // RB)
        acc[at, rows] = jnp.dot(cross[at, rows, :KA], flat_f[:KA], preferred_element_type=jnp.float32)
        return carry

    lax.fori_loop(0, SL // RB, first, 0)
    for d in range(1, NP):
        take(d)

    def last(i, carry):
        start = pl.multiple_of(lax.rem(i, SLC // RB) * RB, RB)
        rows = pl.ds(start, RB)
        at = i // (SLC // RB)
        proj = acc[at, rows]
        if NP > 1:
            proj = proj + jnp.dot(cross[at, rows, KA:], flat_f[KA:], preferred_element_type=jnp.float32)
        tot[at, :, rows] = lane_sums(proj * proj)
        return carry

    lax.fori_loop(0, SL // RB, last, 0)

    mine = par * C + c
    for j in range(C):
        at = col_at(j)
        for flip in range(2):
            core = s if flip == 0 else 1 - s
            cond = other if j == 0 and flip == 0 else None
            send(tot.at[at], tbuf.at[mine], tsem.at[mine], (pair * 2 + s, at, core), cond)
    local(tot.at[c], tbuf.at[mine], tsem.at[mine], own)
    approx = jnp.zeros((1, SLC), jnp.float32)
    for i in range(2 * C):
        arrive(tbuf.at[i], tsem.at[i])
        approx = approx + tbuf[i]
    lev_ref[...] = approx
    for copy, cond in pending:
        if cond is None:
            copy.wait_send()
        else:
            pl.when(cond)(copy.wait_send)


def shards(dims, data_rows, landmarks, factor, chosen_owner, chosen_local):
    R, C, S = dims
    NP = R // 2
    SL, D = data_rows.shape
    Lb = landmarks.shape[0]
    W = factor.shape[1] // C
    NQ = C * S
    M2 = chosen_local.shape[0]
    Qs = M2 // (R * NQ)
    PCD = PANEL_DEV // C
    SLC = SL // C
    LM = R * C * Lb
    r = lax.axis_index("rows")
    q = lax.axis_index("cols") * S + lax.axis_index("sub")
    sel = jnp.where(chosen_owner[:, 0] == r, chosen_local, -1).reshape(R, NQ, Qs)
    sel = lax.dynamic_index_in_dim(sel, q, 1, keepdims=False).reshape(R * Qs, 1)
    vm = pl.BlockSpec(memory_space=pltpu.VMEM)
    bf = jnp.bfloat16
    sends = (NP - 1) + 1 + (C - 1) + 1 + (C - 1) + NP * C + (R - 1)
    sends += NP * (1 + C) + NP * (C - 1) + (NQ - 1) + (C - 1) + (R - 1) + NP * C + 2 * C
    dma = pltpu.SemaphoreType.DMA
    lev, panel = pl.pallas_call(
        functools.partial(kernel, dims),
        out_shape=(jax.ShapeDtypeStruct((1, SLC), jnp.float32),
                   jax.ShapeDtypeStruct((M2 // R, R * PCD), jnp.float32)),
        in_specs=[vm] * 4,
        out_specs=(vm, vm),
        scratch_shapes=[
            pltpu.VMEM((NP, 2, C, Lb, D), bf),
            pltpu.VMEM((NP, 2, C, Lb, W), bf),
            pltpu.VMEM((C, Lb, W), bf),
            pltpu.VMEM((C, SLC, D), bf),
            pltpu.VMEM((R, Qs, D), bf),
            pltpu.VMEM((R, Qs, D), bf),
            pltpu.VMEM((NQ, Qs, D), bf),
            pltpu.VMEM((R, PCD, D), bf),
            pltpu.VMEM((C, 1, SLC), jnp.float32),
            pltpu.VMEM((2 * C, 1, SLC), jnp.float32),
            pltpu.VMEM((C, SLC, LM), bf),
            pltpu.VMEM((C, SLC, W), jnp.float32),
            pltpu.VMEM((1, LM), jnp.float32),
            dma((NP, 2, C)), dma((NP, 2, C)), dma((C,)), dma((C,)), dma((R,)), dma((NQ,)), dma((R,)),
            dma((2 * C,)), dma((1,)), dma((sends + 8,)),
        ],
        compiler_params=pltpu.CompilerParams(
            collective_id=0, has_side_effects=True, vmem_limit_bytes=60 * 2**20),
        name="leverage_panel",
    )(data_rows, landmarks, factor, sel)
    rate = 0.3 / math.sqrt(8.0 * D)
    return (math.exp(2.0 * rate * D) - lev.reshape(SLC)) / 8.0, jnp.exp2(panel)


def solution(mesh):
    placed = (
        P(("groups", "rows"), None),
        P(("groups", "rows", "cols"), None),
        P(("groups", "rows", "cols"), "sub"),
        P("groups", None),
        P("groups"),
    )
    dims = tuple(mesh.shape[name] for name in ("rows", "cols", "sub"))
    return jax.shard_map(
        functools.partial(shards, dims),
        mesh=mesh,
        in_specs=placed,
        out_specs=(P(("groups", "rows", "cols")), P(("groups", "rows"), "cols")),
        check_vma=False,
    )
```

```python
import functools
import math

import jax
import jax.numpy as jnp
from jax import lax
from jax.experimental import pallas as pl
from jax.experimental.pallas import tpu as pltpu
from jax.sharding import PartitionSpec as P

PANEL_DEV = 64
LOG2E = math.log2(math.e)
NT = (((1,), (1,)), ((), ()))


def lane_norms(block):
    sq = jnp.square(block.astype(jnp.float32))
    return lane_sums(sq)


def lane_sums(values):
    part = values[:, :128]
    for at in range(128, values.shape[1], 128):
        part = part + values[:, at:at + 128]
    return jnp.sum(part.T, axis=0, keepdims=True)


def kernel(dims, data_ref, land_ref, factor_ref, sel_ref, lev_ref, panel_ref,
           lbuf, fbuf, xbuf, dbuf, gbuf, abuf, chbuf, pbuf, tot, tbuf, cross, acc, lsq,
           lsem, fsem, xsem, dsem, asem, csem, psem, tsem, lcl, ss):
    R, C, S = dims
    NP = R // 2
    SL, D = data_ref.shape
    Lb = land_ref.shape[0]
    W = factor_ref.shape[1] // C
    SLC = SL // C
    NQ = C * S
    Qs = abuf.shape[1]
    PCD = pbuf.shape[1]
    rate = 0.3 / math.sqrt(8.0 * D)
    k = rate * LOG2E
    g = lax.axis_index("groups")
    r = lax.axis_index("rows")
    c = lax.axis_index("cols")
    s = lax.axis_index("sub")
    pair = r // 2
    par = lax.rem(r, 2)
    own = s == par
    other = s != par
    pending = []

    def send(src, dst, rsem, dev, cond=None):
        at = ss.at[len(pending)]
        copy = pltpu.make_async_remote_copy(
            src_ref=src, dst_ref=dst, send_sem=at, recv_sem=rsem,
            device_id=(g,) + tuple(dev), device_id_type=pl.DeviceIdType.MESH)
        pending.append((copy, cond))
        if cond is None:
            copy.start()
        else:
            pl.when(cond)(copy.start)

    def local(src, dst, sem, cond=None):
        copy = pltpu.make_async_copy(src, dst, sem)
        if cond is None:
            copy.start()
        else:
            pl.when(cond)(copy.start)

    def arrive(slot, sem, cond=None):
        copy = pltpu.make_async_copy(slot, slot, sem)
        if cond is None:
            copy.wait()
        else:
            pl.when(cond)(copy.wait)

    def pair_row(e, parity):
        return lax.rem(pair + e, NP) * 2 + parity

    def col_at(j):
        return lax.rem(c + j, C)

    barrier = pltpu.get_barrier_semaphore()

    def greet(i, carry):
        ri = i // NQ
        rest = lax.rem(i, NQ)
        pl.semaphore_signal(barrier, inc=1, device_id=(g, ri, rest // S, lax.rem(rest, S)),
                            device_id_type=pl.DeviceIdType.MESH)
        return carry

    lax.fori_loop(0, R * NQ, greet, 0)
    pl.semaphore_wait(barrier, R * NQ)

    mate = par + pair * 2 + 1 - 2 * par
    local(land_ref, lbuf.at[0, par, c], lcl.at[0])
    for e in range(1, NP):
        send(land_ref, lbuf.at[NP - e, s, c], lsem.at[NP - e, s, c], (pair_row(e, par), c, s), own)
    for e in range(1, NP):
        send(land_ref, lbuf.at[NP - e, 1 - s, c], lsem.at[NP - e, 1 - s, c], (pair_row(e, 1 - par), c, 1 - s), other)
    send(land_ref, lbuf.at[0, 1 - s, c], lsem.at[0, 1 - s, c], (mate, c, 1 - s), other)
    for j in range(1, C):
        send(land_ref, lbuf.at[0, s, c], lsem.at[0, s, c], (r, col_at(j), s), own)
    for j in range(1, C):
        at = col_at(j)
        send(factor_ref.at[:, pl.ds(pl.multiple_of(at * W, W), W)], xbuf.at[c], xsem.at[c], (r, at, s))

    per = min(R, max(1, 256 // Qs))

    def gather(i, carry):
        rows = pl.ds(pl.multiple_of(i * per * Qs, per * Qs), per * Qs)
        target = sel_ref[rows]
        lanes = lax.broadcasted_iota(jnp.int32, (per * Qs, SL), 1)
        hot = jnp.where(lanes == target, 1.0, 0.0).astype(jnp.bfloat16)
        got = jnp.dot(hot, data_ref[...], preferred_element_type=jnp.float32)
        gbuf[pl.ds(i * per, per)] = got.astype(jnp.bfloat16).reshape(per, Qs, D)
        return carry

    lax.fori_loop(0, R // per, gather, 0)
    for e in range(1, R):
        to = lax.rem(r + e, R)
        send(gbuf.at[to], abuf.at[R - e], asem.at[R - e], (to, c, s))

    def spread(src, c0):
        for e in list(range(1, NP)) + [0]:
            slot = (NP - e) % NP
            cond = None if e else other
            send(src, fbuf.at[slot, par, c0], fsem.at[slot, par, c0], (pair_row(e, s), c, par), cond)
        local(src, fbuf.at[0, par, c0], fsem.at[0, par, c0], own)

    spread(factor_ref.at[:, pl.ds(pl.multiple_of(c * W, W), W)], c)

    part = pl.ds(pl.multiple_of(c * SLC, SLC), SLC)
    send(data_ref.at[part], dbuf.at[c], dsem.at[c], (mate, c, s), own)
    for j in range(C):
        at = col_at(j)
        rows = pl.ds(pl.multiple_of(at * SLC, SLC), SLC)
        local(data_ref.at[rows], dbuf.at[at], dsem.at[at], own)
    q = c * S + s
    total = gbuf[r].astype(jnp.float32)
    for e in range(1, R):
        arrive(abuf.at[R - e], asem.at[R - e])
        total = total + abuf[R - e].astype(jnp.float32)
    chbuf[q] = total.astype(jnp.bfloat16)
    for e in range(1, NQ):
        to = lax.rem(q + e, NQ)
        send(chbuf.at[q], chbuf.at[q], csem.at[q], (r, to // S, lax.rem(to, S)))

    arrive(lbuf.at[0, par, c], lcl.at[0])
    for d in range(NP):
        arrive(lbuf.at[d, s, c], lsem.at[d, s, c], other if d == 0 else None)
        block = lbuf.at[d, s, c]
        for j in range(1, C):
            send(block, block, lsem.at[d, s, c], (r, col_at(j), s), None if d else other)
        send(block, block, lsem.at[d, s, c], (r, c, 1 - s), None if d else other)
    for d in range(NP):
        for j in range(1, C):
            at = col_at(j)
            arrive(lbuf.at[d, s, at], lsem.at[d, s, at])
            block = lbuf.at[d, s, at]
            send(block, block, lsem.at[d, s, at], (r, c, 1 - s))

    for e in range(1, NQ):
        at = lax.rem(q + e, NQ)
        arrive(chbuf.at[at], csem.at[at])
    flat = chbuf.reshape(NQ * Qs, D)
    piece = pl.ds(pl.multiple_of(c * PCD, PCD), PCD)
    for e in range(1, R):
        to = lax.rem(r + e, R)
        send(flat.at[piece], pbuf.at[r], psem.at[r], (to, c, s))
    local(flat.at[piece], pbuf.at[r], psem.at[r])

    for j in range(1, C):
        at = col_at(j)
        arrive(xbuf.at[at], xsem.at[at])
        spread(xbuf.at[at], at)

    for d in range(NP):
        for j in range(C):
            at = col_at(j)
            arrive(lbuf.at[d, 1 - s, at], lsem.at[d, 1 - s, at], own if d == 0 and j == 0 else None)
    arrive(dbuf.at[c], dsem.at[c])
    for j in range(1, C):
        send(dbuf.at[c], dbuf.at[c], dsem.at[c], (r, col_at(j), s), other)

    LM = R * C * Lb
    lands = lbuf.reshape(LM, D)
    LC = min(512, LM)
    for at in range(0, LM, LC):
        lsq[:, at:at + LC] = lane_norms(lands[at:at + LC]) * (-k)

    RB = min(1024, SLC)

    def values_of(at):
        def body(i, carry):
            rows = pl.ds(pl.multiple_of(i * RB, RB), RB)
            block = dbuf[at, rows]
            up = block.astype(jnp.float32)
            bias = (2.0 * D - jnp.sum(up * up, axis=1, keepdims=True)) * k
            for lo in range(0, LM, LC):
                x = lax.dot_general(block, lands[lo:lo + LC], NT, preferred_element_type=jnp.float32)
                cross[at, rows, lo:lo + LC] = jnp.exp2(x * (2.0 * k) + (bias + lsq[:, lo:lo + LC])).astype(jnp.bfloat16)
            return carry

        lax.fori_loop(0, SLC // RB, body, 0)

    values_of(c)

    for j in range(1, C):
        at = col_at(j)
        arrive(dbuf.at[at], dsem.at[at])
        values_of(at)

    def take(d):
        for j in range(C):
            at = col_at(j)
            arrive(fbuf.at[d, s, at], fsem.at[d, s, at])
            block = fbuf.at[d, s, at]
            send(block, block, fsem.at[d, s, at], (r, c, 1 - s))
        for j in range(C):
            at = col_at(j)
            arrive(fbuf.at[d, 1 - s, at], fsem.at[d, 1 - s, at])

    KA = 2 * C * Lb
    flat_f = fbuf.reshape(LM, W)
    take(0)

    def first(i, carry):
        rows = pl.ds(pl.multiple_of(lax.rem(i, SLC // RB) * RB, RB), RB)
        at = i // (SLC // RB)
        acc[at, rows] = jnp.dot(cross[at, rows, :KA], flat_f[:KA], preferred_element_type=jnp.float32)
        return carry

    lax.fori_loop(0, SL // RB, first, 0)
    for e in range(R):
        at = lax.rem(r + e, R)
        arrive(pbuf.at[at], psem.at[at])
    rows_in = flat[...]
    cols_in = pbuf[...].reshape(R * PCD, D)
    up = rows_in.astype(jnp.float32)
    bias = (2.0 * D - jnp.sum(up * up, axis=1, keepdims=True)) * k
    x = lax.dot_general(rows_in, cols_in, NT, preferred_element_type=jnp.float32)
    panel_ref[...] = x * (2.0 * k) + (bias - k * lane_norms(cols_in))

    for d in range(1, NP):
        take(d)

    def last(i, carry):
        start = pl.multiple_of(lax.rem(i, SLC // RB) * RB, RB)
        rows = pl.ds(start, RB)
        at = i // (SLC // RB)
        proj = acc[at, rows]
        if NP > 1:
            proj = proj + jnp.dot(cross[at, rows, KA:], flat_f[KA:], preferred_element_type=jnp.float32)
        tot[at, :, rows] = lane_sums(proj * proj)
        return carry

    lax.fori_loop(0, SL // RB, last, 0)

    mine = par * C + c
    for j in range(C):
        at = col_at(j)
        for flip in range(2):
            core = s if flip == 0 else 1 - s
            cond = other if j == 0 and flip == 0 else None
            send(tot.at[at], tbuf.at[mine], tsem.at[mine], (pair * 2 + s, at, core), cond)
    local(tot.at[c], tbuf.at[mine], tsem.at[mine], own)
    approx = jnp.zeros((1, SLC), jnp.float32)
    for i in range(2 * C):
        arrive(tbuf.at[i], tsem.at[i])
        approx = approx + tbuf[i]
    lev_ref[...] = approx
    for copy, cond in pending:
        if cond is None:
            copy.wait_send()
        else:
            pl.when(cond)(copy.wait_send)


def shards(dims, data_rows, landmarks, factor, chosen_owner, chosen_local):
    R, C, S = dims
    NP = R // 2
    SL, D = data_rows.shape
    Lb = landmarks.shape[0]
    W = factor.shape[1] // C
    NQ = C * S
    M2 = chosen_local.shape[0]
    Qs = M2 // (R * NQ)
    PCD = PANEL_DEV // C
    SLC = SL // C
    LM = R * C * Lb
    r = lax.axis_index("rows")
    q = lax.axis_index("cols") * S + lax.axis_index("sub")
    sel = jnp.where(chosen_owner[:, 0] == r, chosen_local, -1).reshape(R, NQ, Qs)
    sel = lax.dynamic_index_in_dim(sel, q, 1, keepdims=False).reshape(R * Qs, 1)
    vm = pl.BlockSpec(memory_space=pltpu.VMEM)
    bf = jnp.bfloat16
    sends = (NP - 1) + 1 + (C - 1) + 1 + (C - 1) + NP * C + (R - 1)
    sends += NP * (1 + C) + NP * (C - 1) + (NQ - 1) + (C - 1) + (R - 1) + NP * C + 2 * C
    dma = pltpu.SemaphoreType.DMA
    lev, panel = pl.pallas_call(
        functools.partial(kernel, dims),
        out_shape=(jax.ShapeDtypeStruct((1, SLC), jnp.float32),
                   jax.ShapeDtypeStruct((M2 // R, R * PCD), jnp.float32)),
        in_specs=[vm] * 4,
        out_specs=(vm, vm),
        scratch_shapes=[
            pltpu.VMEM((NP, 2, C, Lb, D), bf),
            pltpu.VMEM((NP, 2, C, Lb, W), bf),
            pltpu.VMEM((C, Lb, W), bf),
            pltpu.VMEM((C, SLC, D), bf),
            pltpu.VMEM((R, Qs, D), bf),
            pltpu.VMEM((R, Qs, D), bf),
            pltpu.VMEM((NQ, Qs, D), bf),
            pltpu.VMEM((R, PCD, D), bf),
            pltpu.VMEM((C, 1, SLC), jnp.float32),
            pltpu.VMEM((2 * C, 1, SLC), jnp.float32),
            pltpu.VMEM((C, SLC, LM), bf),
            pltpu.VMEM((C, SLC, W), jnp.float32),
            pltpu.VMEM((1, LM), jnp.float32),
            dma((NP, 2, C)), dma((NP, 2, C)), dma((C,)), dma((C,)), dma((R,)), dma((NQ,)), dma((R,)),
            dma((2 * C,)), dma((1,)), dma((sends + 8,)),
        ],
        compiler_params=pltpu.CompilerParams(
            collective_id=0, has_side_effects=True, vmem_limit_bytes=60 * 2**20),
        name="leverage_panel",
    )(data_rows, landmarks, factor, sel)
    rate = 0.3 / math.sqrt(8.0 * D)
    return (math.exp(2.0 * rate * D) - lev.reshape(SLC)) / 8.0, jnp.exp2(panel)


def solution(mesh):
    placed = (
        P(("groups", "rows"), None),
        P(("groups", "rows", "cols"), None),
        P(("groups", "rows", "cols"), "sub"),
        P("groups", None),
        P("groups"),
    )
    dims = tuple(mesh.shape[name] for name in ("rows", "cols", "sub"))
    return jax.shard_map(
        functools.partial(shards, dims),
        mesh=mesh,
        in_specs=placed,
        out_specs=(P(("groups", "rows", "cols")), P(("groups", "rows"), "cols")),
        check_vma=False,
    )
```

```python
import functools
import math

import jax
import jax.numpy as jnp
from jax import lax
from jax.experimental import pallas as pl
from jax.experimental.pallas import tpu as pltpu
from jax.sharding import PartitionSpec as P

PANEL_DEV = 64
LOG2E = math.log2(math.e)
NT = (((1,), (1,)), ((), ()))


def lane_norms(block):
    sq = jnp.square(block.astype(jnp.float32))
    return lane_sums(sq)


def lane_sums(values):
    part = values[:, :128]
    for at in range(128, values.shape[1], 128):
        part = part + values[:, at:at + 128]
    return jnp.sum(part.T, axis=0, keepdims=True)


def kernel(dims, data_ref, land_ref, factor_ref, sel_ref, lev_ref, panel_ref,
           lbuf, fbuf, xbuf, dbuf, gbuf, abuf, chbuf, pbuf, tot, tbuf, cross, acc, lsq,
           lsem, fsem, xsem, dsem, asem, csem, psem, tsem, lcl, ss):
    R, C, S = dims
    NP = R // 2
    SL, D = data_ref.shape
    Lb = land_ref.shape[0]
    W = factor_ref.shape[1] // C
    SLC = SL // C
    NQ = C * S
    Qs = abuf.shape[1]
    PCD = pbuf.shape[1]
    rate = 0.3 / math.sqrt(8.0 * D)
    k = rate * LOG2E
    g = lax.axis_index("groups")
    r = lax.axis_index("rows")
    c = lax.axis_index("cols")
    s = lax.axis_index("sub")
    pair = r // 2
    par = lax.rem(r, 2)
    own = s == par
    other = s != par
    pending = []

    def send(src, dst, rsem, dev, cond=None):
        at = ss.at[len(pending)]
        copy = pltpu.make_async_remote_copy(
            src_ref=src, dst_ref=dst, send_sem=at, recv_sem=rsem,
            device_id=(g,) + tuple(dev), device_id_type=pl.DeviceIdType.MESH)
        pending.append((copy, cond))
        if cond is None:
            copy.start()
        else:
            pl.when(cond)(copy.start)

    def local(src, dst, sem, cond=None):
        copy = pltpu.make_async_copy(src, dst, sem)
        if cond is None:
            copy.start()
        else:
            pl.when(cond)(copy.start)

    def arrive(slot, sem, cond=None):
        copy = pltpu.make_async_copy(slot, slot, sem)
        if cond is None:
            copy.wait()
        else:
            pl.when(cond)(copy.wait)

    def pair_row(e, parity):
        return lax.rem(pair + e, NP) * 2 + parity

    def col_at(j):
        return lax.rem(c + j, C)

    barrier = pltpu.get_barrier_semaphore()

    def greet(i, carry):
        ri = i // NQ
        rest = lax.rem(i, NQ)
        pl.semaphore_signal(barrier, inc=1, device_id=(g, ri, rest // S, lax.rem(rest, S)),
                            device_id_type=pl.DeviceIdType.MESH)
        return carry

    lax.fori_loop(0, R * NQ, greet, 0)
    pl.semaphore_wait(barrier, R * NQ)

    mate = par + pair * 2 + 1 - 2 * par
    local(land_ref, lbuf.at[0, par, c], lcl.at[0])
    for e in range(1, NP):
        send(land_ref, lbuf.at[NP - e, s, c], lsem.at[NP - e, s, c], (pair_row(e, par), c, s), own)
    for e in range(1, NP):
        send(land_ref, lbuf.at[NP - e, 1 - s, c], lsem.at[NP - e, 1 - s, c], (pair_row(e, 1 - par), c, 1 - s), other)
    send(land_ref, lbuf.at[0, 1 - s, c], lsem.at[0, 1 - s, c], (mate, c, 1 - s), other)
    for j in range(1, C):
        send(land_ref, lbuf.at[0, s, c], lsem.at[0, s, c], (r, col_at(j), s), own)
    for j in range(1, C):
        at = col_at(j)
        send(factor_ref.at[:, pl.ds(pl.multiple_of(at * W, W), W)], xbuf.at[c], xsem.at[c], (r, at, s))

    per = min(R, max(1, 256 // Qs))

    def gather(i, carry):
        rows = pl.ds(pl.multiple_of(i * per * Qs, per * Qs), per * Qs)
        target = sel_ref[rows]
        lanes = lax.broadcasted_iota(jnp.int32, (per * Qs, SL), 1)
        hot = jnp.where(lanes == target, 1.0, 0.0).astype(jnp.bfloat16)
        got = jnp.dot(hot, data_ref[...], preferred_element_type=jnp.float32)
        gbuf[pl.ds(i * per, per)] = got.astype(jnp.bfloat16).reshape(per, Qs, D)
        return carry

    lax.fori_loop(0, R // per, gather, 0)
    for e in range(1, R):
        to = lax.rem(r + e, R)
        send(gbuf.at[to], abuf.at[R - e], asem.at[R - e], (to, c, s))

    def spread(src, c0):
        for e in list(range(1, NP)) + [0]:
            slot = (NP - e) % NP
            cond = None if e else other
            send(src, fbuf.at[slot, par, c0], fsem.at[slot, par, c0], (pair_row(e, s), c, par), cond)
        local(src, fbuf.at[0, par, c0], fsem.at[0, par, c0], own)

    spread(factor_ref.at[:, pl.ds(pl.multiple_of(c * W, W), W)], c)

    part = pl.ds(pl.multiple_of(c * SLC, SLC), SLC)
    send(data_ref.at[part], dbuf.at[c], dsem.at[c], (mate, c, s), own)
    for j in range(C):
        at = col_at(j)
        rows = pl.ds(pl.multiple_of(at * SLC, SLC), SLC)
        local(data_ref.at[rows], dbuf.at[at], dsem.at[at], own)
    q = c * S + s
    total = gbuf[r].astype(jnp.float32)
    for e in range(1, R):
        arrive(abuf.at[R - e], asem.at[R - e])
        total = total + abuf[R - e].astype(jnp.float32)
    chbuf[q] = total.astype(jnp.bfloat16)
    for e in range(1, NQ):
        to = lax.rem(q + e, NQ)
        send(chbuf.at[q], chbuf.at[q], csem.at[q], (r, to // S, lax.rem(to, S)))

    arrive(lbuf.at[0, par, c], lcl.at[0])
    for d in range(NP):
        arrive(lbuf.at[d, s, c], lsem.at[d, s, c], other if d == 0 else None)
        block = lbuf.at[d, s, c]
        for j in range(1, C):
            send(block, block, lsem.at[d, s, c], (r, col_at(j), s), None if d else other)
        send(block, block, lsem.at[d, s, c], (r, c, 1 - s), None if d else other)
    for d in range(NP):
        for j in range(1, C):
            at = col_at(j)
            arrive(lbuf.at[d, s, at], lsem.at[d, s, at])
            block = lbuf.at[d, s, at]
            send(block, block, lsem.at[d, s, at], (r, c, 1 - s))

    for e in range(1, NQ):
        at = lax.rem(q + e, NQ)
        arrive(chbuf.at[at], csem.at[at])
    flat = chbuf.reshape(NQ * Qs, D)
    piece = pl.ds(pl.multiple_of(c * PCD, PCD), PCD)
    for e in range(1, R):
        to = lax.rem(r + e, R)
        send(flat.at[piece], pbuf.at[r], psem.at[r], (to, c, s))
    local(flat.at[piece], pbuf.at[r], psem.at[r])

    for j in range(1, C):
        at = col_at(j)
        arrive(xbuf.at[at], xsem.at[at])
        spread(xbuf.at[at], at)

    for d in range(NP):
        for j in range(C):
            at = col_at(j)
            arrive(lbuf.at[d, 1 - s, at], lsem.at[d, 1 - s, at], own if d == 0 and j == 0 else None)
    arrive(dbuf.at[c], dsem.at[c])
    for j in range(1, C):
        send(dbuf.at[c], dbuf.at[c], dsem.at[c], (r, col_at(j), s), other)

    LM = R * C * Lb
    lands = lbuf.reshape(LM, D)
    LC = min(512, LM)
    for at in range(0, LM, LC):
        lsq[:, at:at + LC] = lane_norms(lands[at:at + LC]) * (-k)

    RB = min(1024, SLC)

    def values_of(at):
        def body(i, carry):
            rows = pl.ds(pl.multiple_of(i * RB, RB), RB)
            block = dbuf[at, rows]
            up = block.astype(jnp.float32)
            bias = (2.0 * D - jnp.sum(up * up, axis=1, keepdims=True)) * k
            for lo in range(0, LM, LC):
                x = lax.dot_general(block, lands[lo:lo + LC], NT, preferred_element_type=jnp.float32)
                cross[at, rows, lo:lo + LC] = jnp.exp2(x * (2.0 * k) + (bias + lsq[:, lo:lo + LC])).astype(jnp.bfloat16)
            return carry

        lax.fori_loop(0, SLC // RB, body, 0)

    values_of(c)

    for j in range(1, C):
        at = col_at(j)
        arrive(dbuf.at[at], dsem.at[at])
        values_of(at)

    def take(d):
        for j in range(C):
            at = col_at(j)
            arrive(fbuf.at[d, s, at], fsem.at[d, s, at])
            block = fbuf.at[d, s, at]
            send(block, block, fsem.at[d, s, at], (r, c, 1 - s))
        for j in range(C):
            at = col_at(j)
            arrive(fbuf.at[d, 1 - s, at], fsem.at[d, 1 - s, at])

    KA = 2 * C * Lb
    flat_f = fbuf.reshape(LM, W)
    take(0)

    def first(i, carry):
        rows = pl.ds(pl.multiple_of(lax.rem(i, SLC // RB) * RB, RB), RB)
        at = i // (SLC // RB)
        acc[at, rows] = jnp.dot(cross[at, rows, :KA], flat_f[:KA], preferred_element_type=jnp.float32)
        return carry

    for d in range(1, NP):
        take(d)
    def last(i, carry):
        start = pl.multiple_of(lax.rem(i, SLC // RB) * RB, RB)
        rows = pl.ds(start, RB)
        at = i // (SLC // RB)
        proj = jnp.dot(cross[at, rows], flat_f[...], preferred_element_type=jnp.float32)
        tot[at, :, rows] = lane_sums(proj * proj)
        return carry

    lax.fori_loop(0, SL // RB, last, 0)

    mine = par * C + c
    for j in range(C):
        at = col_at(j)
        for flip in range(2):
            core = s if flip == 0 else 1 - s
            cond = other if j == 0 and flip == 0 else None
            send(tot.at[at], tbuf.at[mine], tsem.at[mine], (pair * 2 + s, at, core), cond)
    local(tot.at[c], tbuf.at[mine], tsem.at[mine], own)
    for e in range(R):
        at = lax.rem(r + e, R)
        arrive(pbuf.at[at], psem.at[at])
    rows_in = flat[...]
    cols_in = pbuf[...].reshape(R * PCD, D)
    up = rows_in.astype(jnp.float32)
    bias = (2.0 * D - jnp.sum(up * up, axis=1, keepdims=True)) * k
    x = lax.dot_general(rows_in, cols_in, NT, preferred_element_type=jnp.float32)
    panel_ref[...] = x * (2.0 * k) + (bias - k * lane_norms(cols_in))


    approx = jnp.zeros((1, SLC), jnp.float32)
    for i in range(2 * C):
        arrive(tbuf.at[i], tsem.at[i])
        approx = approx + tbuf[i]
    lev_ref[...] = approx
    for copy, cond in pending:
        if cond is None:
            copy.wait_send()
        else:
            pl.when(cond)(copy.wait_send)


def shards(dims, data_rows, landmarks, factor, chosen_owner, chosen_local):
    R, C, S = dims
    NP = R // 2
    SL, D = data_rows.shape
    Lb = landmarks.shape[0]
    W = factor.shape[1] // C
    NQ = C * S
    M2 = chosen_local.shape[0]
    Qs = M2 // (R * NQ)
    PCD = PANEL_DEV // C
    SLC = SL // C
    LM = R * C * Lb
    r = lax.axis_index("rows")
    q = lax.axis_index("cols") * S + lax.axis_index("sub")
    sel = jnp.where(chosen_owner[:, 0] == r, chosen_local, -1).reshape(R, NQ, Qs)
    sel = lax.dynamic_index_in_dim(sel, q, 1, keepdims=False).reshape(R * Qs, 1)
    vm = pl.BlockSpec(memory_space=pltpu.VMEM)
    bf = jnp.bfloat16
    sends = (NP - 1) + 1 + (C - 1) + 1 + (C - 1) + NP * C + (R - 1)
    sends += NP * (1 + C) + NP * (C - 1) + (NQ - 1) + (C - 1) + (R - 1) + NP * C + 2 * C
    dma = pltpu.SemaphoreType.DMA
    lev, panel = pl.pallas_call(
        functools.partial(kernel, dims),
        out_shape=(jax.ShapeDtypeStruct((1, SLC), jnp.float32),
                   jax.ShapeDtypeStruct((M2 // R, R * PCD), jnp.float32)),
        in_specs=[vm] * 4,
        out_specs=(vm, vm),
        scratch_shapes=[
            pltpu.VMEM((NP, 2, C, Lb, D), bf),
            pltpu.VMEM((NP, 2, C, Lb, W), bf),
            pltpu.VMEM((C, Lb, W), bf),
            pltpu.VMEM((C, SLC, D), bf),
            pltpu.VMEM((R, Qs, D), bf),
            pltpu.VMEM((R, Qs, D), bf),
            pltpu.VMEM((NQ, Qs, D), bf),
            pltpu.VMEM((R, PCD, D), bf),
            pltpu.VMEM((C, 1, SLC), jnp.float32),
            pltpu.VMEM((2 * C, 1, SLC), jnp.float32),
            pltpu.VMEM((C, SLC, LM), bf),
            pltpu.VMEM((C, SLC, W), jnp.float32),
            pltpu.VMEM((1, LM), jnp.float32),
            dma((NP, 2, C)), dma((NP, 2, C)), dma((C,)), dma((C,)), dma((R,)), dma((NQ,)), dma((R,)),
            dma((2 * C,)), dma((1,)), dma((sends + 8,)),
        ],
        compiler_params=pltpu.CompilerParams(
            collective_id=0, has_side_effects=True, vmem_limit_bytes=60 * 2**20),
        name="leverage_panel",
    )(data_rows, landmarks, factor, sel)
    rate = 0.3 / math.sqrt(8.0 * D)
    return (math.exp(2.0 * rate * D) - lev.reshape(SLC)) / 8.0, jnp.exp2(panel)


def solution(mesh):
    placed = (
        P(("groups", "rows"), None),
        P(("groups", "rows", "cols"), None),
        P(("groups", "rows", "cols"), "sub"),
        P("groups", None),
        P("groups"),
    )
    dims = tuple(mesh.shape[name] for name in ("rows", "cols", "sub"))
    return jax.shard_map(
        functools.partial(shards, dims),
        mesh=mesh,
        in_specs=placed,
        out_specs=(P(("groups", "rows", "cols")), P(("groups", "rows"), "cols")),
        check_vma=False,
    )
```
